256 devices in a mesh: gx: 16 (over x, y), gy: 16 (over z, core).
Axes of the slice: x: 4, y: 4, z: 8, core: 2. Of those that a mesh axis runs over, the one named last changes fastest.
Arguments:
- density: float32 [8, 128, 32768], P(None, 'gy', 'gx'), may hold values from 0.04 to 80, as said below
- drift: float32 [2, 128, 32768], P(None, 'gy', 'gx'), may hold values from -0.1 to 0.1
- kill: float32 [128, 32768], P('gy', 'gx'), may hold values from 0.02 to 0.1
- diffusion: float32 [8], replicated, may hold values from 0.05 to 0.1
- jump_rate: float32 [8], replicated, may hold values from 0.1 to 0.5
- kernel_vals: float32 [8, 8192], replicated, may hold values from 0.001 to 1
- jump_len: int32 [8], replicated, may hold values from 2048 to 8192
- rate_table: float32 [64], replicated, may hold values from 0.002 to 0.035
- rate_index: int32 [8, 8], replicated, may hold values from 0 to 63
Outputs:
- density_out: float32 [8, 128, 32768], P(None, 'gy', 'gx')
The draws below stay inside these ranges and needn't reach their ends.
Inputs may be any that keep to these rules, and one draw needn't show every extreme that they name: Every density is positive.
All inputs are finite; a program needn't handle non-finite values.
Results may differ from the reference program's by a relative error of at most 0.0001.
Values sent between devices are 32-bit elements; how exact they have to be, the bound alone decides.
A program may use at most 64 MiB of HBM per device.

```python
import math
import jax
import jax.numpy as jnp
from jax import lax

R = 8
NX = 32768
JMAX = 8192
NT = 64
SWEEPS = 2
NY = 128


def draw_density(key, part):
    shape = (R, NY, NX)
    key_amp = jax.random.fold_in(key, 21)
    key_shift = jax.random.fold_in(key, 22)
    key_noise = jax.random.fold_in(key, 23)
    x_int = lax.broadcasted_iota(jnp.int32, shape, 2)
    rising = 1.0 + 2.0 * x_int.astype(jnp.float32) / NX
    levels = 9
    amp_top = 0.3
    amps = jax.random.uniform(key_amp, (levels, R, NY, 1), jnp.float32, -amp_top, amp_top)
    shifts = jax.random.randint(key_shift, (levels, R, NY, 1), 0, 4096)
    log_field = jnp.zeros(shape, jnp.float32)
    for level in range(levels):
        wave = 16 * 2 ** level
        phase = ((x_int + shifts[level]) % wave).astype(jnp.float32) * (2.0 * math.pi / wave)
        log_field = log_field + amps[level] * jnp.sin(phase)
    noise = jnp.exp(jax.random.uniform(key_noise, shape, jnp.float32, -0.5, 0.5))
    return jnp.exp(log_field) * noise * rising


def draw_jump_len(key, part):
    key_vals = jax.random.fold_in(key, 11)
    key_top = jax.random.fold_in(key, 12)
    key_low = jax.random.fold_in(key, 13)
    lengths = jax.random.randint(key_vals, (R,), JMAX // 4, JMAX + 1)
    top_slot = jax.random.randint(key_top, (), 0, R)
    low_slot = (top_slot + 1 + jax.random.randint(key_low, (), 0, R - 1)) % R
    slots = jnp.arange(R, dtype=jnp.int32)
    lengths = jnp.where(slots == top_slot, JMAX, lengths)
    lengths = jnp.where(slots == low_slot, JMAX // 4, lengths)
    return lengths.astype(jnp.int32)


def with_ends(values, key, low, high):
    longest = values.shape.index(max(values.shape))
    spots = []
    for shift in (0, 1):
        where = [jax.random.randint(jax.random.fold_in(key, axis), (), 0, length) for axis, length in enumerate(values.shape)]
        where[longest] = (where[longest] + shift) % values.shape[longest]
        spots.append(tuple(where))
    return values.at[spots[0]].set(low).at[spots[1]].set(high)


def steps_of(key, shape, shards, smallest, high):
    factor_of = 1.0
    for position, shards_of in shards:
        heights = jax.random.uniform(jax.random.fold_in(jax.random.fold_in(key, 6), position), (shards_of,), jnp.float32, smallest / len(shards), high / len(shards))
        factor_of = factor_of * jnp.repeat(jnp.exp(heights), shape[position] // shards_of).reshape((-1,) + (1,) * (len(shape) - 1 - position))
    return factor_of


def setup_inputs(seed: int = 0) -> dict:
    arg_keys = jax.random.split(jax.random.key(seed), 10)
    return {
        "density": draw_density(jax.random.fold_in(arg_keys[9], 71), 0),
        "drift": jnp.clip(jax.random.uniform(arg_keys[1], (2, NY, NX), jnp.float32, -0.1, 0.1) * steps_of(arg_keys[1], (2, NY, NX), ((1, 16), (2, 16)), -0.4, 0.0), -0.1, 0.1),
        "kill": jnp.clip(jnp.exp(math.log(0.1) - 1.609438 * jax.random.uniform(arg_keys[2], (NY, NX), jnp.float32) ** steps_of(arg_keys[2], (NY, NX), ((0, 16), (1, 16)), -0.2, 0.2)), 0.02, 0.1),
        "diffusion": jnp.clip(jnp.exp(jax.random.uniform(arg_keys[3], (R,), jnp.float32, math.log(0.05), math.log(0.1))), 0.05, 0.1),
        "jump_rate": jnp.clip(jnp.exp(jax.random.uniform(arg_keys[4], (R,), jnp.float32, math.log(0.1), math.log(0.5))), 0.1, 0.5),
        "kernel_vals": jnp.clip(jnp.exp(jax.random.uniform(arg_keys[5], (R, JMAX), jnp.float32, math.log(0.001), math.log(1.0))), 0.001, 1.0),
        "jump_len": draw_jump_len(jax.random.fold_in(arg_keys[9], 71), 0),
        "rate_table": jnp.clip(jnp.exp(jax.random.uniform(arg_keys[7], (NT,), jnp.float32, math.log(0.002), math.log(0.035))), 0.002, 0.035),
        "rate_index": with_ends(jax.random.randint(arg_keys[8], (R, R), 0, NT), jax.random.fold_in(arg_keys[8], 1), 0, NT - 1).astype(jnp.int32),
    }


def generator(rate_table, rate_index):
    picked = (rate_index[:, :, None] == jnp.arange(NT, dtype=jnp.int32)[None, None, :]).astype(rate_table.dtype)
    offdiag = jnp.sum(picked * rate_table[None, None, :], axis=2) * (1.0 - jnp.eye(R, dtype=rate_table.dtype))
    return offdiag - jnp.diag(jnp.sum(offdiag, axis=1))


def reference(density, drift, kill, diffusion, jump_rate, kernel_vals, jump_len, rate_table, rate_index):
    float_type = density.dtype
    inside = jnp.arange(JMAX, dtype=jnp.int32)[None, :] < jump_len[:, None]
    weights = jnp.where(inside, kernel_vals, jnp.zeros_like(kernel_vals))
    weights = weights / jnp.sum(weights, axis=1, keepdims=True)
    kernel = jnp.concatenate([jnp.zeros((R, 1), float_type), weights, jnp.zeros((R, NX - JMAX - 1), float_type)], axis=1)
    spectrum = jnp.fft.fft(kernel, axis=1)
    generator_matrix = generator(rate_table, rate_index)

    def transport(packed):
        regime_field, kern_spec, diffuse, jump_coef = packed
        jumped = jnp.real(jnp.fft.ifft(jnp.fft.fft(regime_field, axis=1) * kern_spec[None, :], axis=1)).astype(float_type)
        laplace = (jnp.roll(regime_field, 1, 1) + jnp.roll(regime_field, -1, 1)
                   + jnp.roll(regime_field, 1, 0) + jnp.roll(regime_field, -1, 0) - 4.0 * regime_field)
        flux_x = drift[0] * regime_field
        flux_y = drift[1] * regime_field
        flow_x = (jnp.roll(flux_x, -1, 1) - jnp.roll(flux_x, 1, 1)) * 0.5
        flow_y = (jnp.roll(flux_y, -1, 0) - jnp.roll(flux_y, 1, 0)) * 0.5
        return diffuse * laplace - flow_x - flow_y + jump_coef * (jumped - regime_field)

    field = density
    for sweep_index in range(SWEEPS):
        change = lax.map(transport, (field, spectrum, diffusion, jump_rate))
        mixing = jnp.einsum("rs,ryx->syx", generator_matrix, field, precision=lax.Precision.HIGHEST)
        updated = field + change - kill[None] * field + mixing
        field = updated / jnp.mean(updated)
    return field
```

```python
import math

import jax
import jax.numpy as jnp
from jax import lax
from jax.sharding import PartitionSpec as P

SWEEPS = 2


HIGHEST_PRECISION = lax.Precision.HIGHEST


def with_halo(array, sides, width):
    for axis, dim in sides:
        peers, length = (lax.axis_size(axis), array.shape[dim])
        up = [(i, (i + 1) % peers) for i in range(peers)]
        down = [(j, i) for i, j in up]
        last = lax.slice_in_dim(array, length - width, length, axis=dim)
        leading = lax.slice_in_dim(array, 0, width, axis=dim)
        before = lax.ppermute(last, axis, up)
        after = lax.ppermute(leading, axis, down)
        array = jnp.concatenate([before, array, after], axis=dim)
    return array


def angle_table(height, breadth, period):
    product = (
        lax.broadcasted_iota(jnp.int32, (height, breadth), 0)
        * lax.broadcasted_iota(jnp.int32, (height, breadth), 1)
        % period
    )
    angles = product.astype(jnp.float32) * (2.0 * math.pi / period)
    return (jnp.cos(angles), jnp.sin(angles))


def factor_pair(length):
    low_factor = 1
    factor = 1
    while factor * factor <= length:
        if length % factor == 0:
            low_factor = factor
        factor += 1
    return (low_factor, length // low_factor)


def forward_lines(line_data, tables):
    (cos_a, sin_a), (cos_b, sin_b), (cos_t, sin_t) = tables
    width_a = cos_a.shape[0]
    width_b = cos_b.shape[0]
    line_count = line_data.shape[0]
    blocks = line_data.reshape(line_count, width_a, width_b)
    first_re = jnp.einsum("mab,ak->mkb", blocks, cos_a, precision=HIGHEST_PRECISION)
    first_im = -jnp.einsum("mab,ak->mkb", blocks, sin_a, precision=HIGHEST_PRECISION)
    turned_re = first_re * cos_t + first_im * sin_t
    turned_im = first_im * cos_t - first_re * sin_t
    final_re = jnp.einsum(
        "mkb,bj->mkj", turned_re, cos_b, precision=HIGHEST_PRECISION
    ) + jnp.einsum("mkb,bj->mkj", turned_im, sin_b, precision=HIGHEST_PRECISION)
    final_im = jnp.einsum(
        "mkb,bj->mkj", turned_im, cos_b, precision=HIGHEST_PRECISION
    ) - jnp.einsum("mkb,bj->mkj", turned_re, sin_b, precision=HIGHEST_PRECISION)
    return (final_re, final_im)


def inverse_lines(spec_re, spec_im, tables):
    (cos_a, sin_a), (cos_b, sin_b), (cos_t, sin_t) = tables
    line_count, width_a, width_b = spec_re.shape
    back_re = jnp.einsum("mkj,jb->mkb", spec_re, cos_b, precision=HIGHEST_PRECISION) - jnp.einsum(
        "mkj,jb->mkb", spec_im, sin_b, precision=HIGHEST_PRECISION
    )
    back_im = jnp.einsum("mkj,jb->mkb", spec_re, sin_b, precision=HIGHEST_PRECISION) + jnp.einsum(
        "mkj,jb->mkb", spec_im, cos_b, precision=HIGHEST_PRECISION
    )
    turned_re = back_re * cos_t - back_im * sin_t
    turned_im = back_re * sin_t + back_im * cos_t
    result = jnp.einsum("mkb,ka->mab", turned_re, cos_a, precision=HIGHEST_PRECISION) - jnp.einsum(
        "mkb,ka->mab", turned_im, sin_a, precision=HIGHEST_PRECISION
    )
    return result.reshape(line_count, width_a * width_b) / (width_a * width_b)


def generator(rate_table, rate_index):
    regimes = rate_index.shape[0]
    entries = rate_table.shape[0]
    picked = (rate_index[:, :, None] == lax.iota(jnp.int32, entries)[None, None, :]).astype(
        jnp.float32
    )
    offdiag = jnp.sum(picked * rate_table[None, None, :], axis=2) * (
        1.0 - jnp.eye(regimes, dtype=jnp.float32)
    )
    return offdiag - jnp.diag(jnp.sum(offdiag, axis=1))


def tree_sum(values):
    for axis in ("gx", "gy"):
        peers = lax.axis_size(axis)
        step = 1
        while step < peers:
            pairs = [(i, i ^ step) for i in range(peers)]
            values = values + lax.ppermute(values, axis, pairs)
            step *= 2
    return values


def local(
    density, drift, kill, diffusion, jump_rate, kernel_vals, jump_len, rate_table, rate_index
):
    regimes, y_rows, x_cols = density.shape
    groups = lax.axis_size("gx")
    length = x_cols * groups
    per_dev = regimes * y_rows // groups
    width_a, width_b = factor_pair(length)
    tables = (
        angle_table(width_a, width_a, width_a),
        angle_table(width_b, width_b, width_b),
        angle_table(width_a, width_b, length),
    )
    support = kernel_vals.shape[1]
    inside = lax.broadcasted_iota(jnp.int32, (regimes, support), 1) < jump_len[:, None]
    weights = jnp.where(inside, kernel_vals, jnp.zeros_like(kernel_vals))
    weights = weights / jnp.sum(weights, axis=1, keepdims=True)
    padded = jnp.concatenate(
        [
            jnp.zeros((regimes, 1), jnp.float32),
            weights,
            jnp.zeros((regimes, length - support - 1), jnp.float32),
        ],
        axis=1,
    )
    kern_re, kern_im = forward_lines(padded, tables)
    line_ids = lax.axis_index("gx") * per_dev + lax.iota(jnp.int32, per_dev)
    owner_mask = (line_ids // y_rows)[:, None] == lax.iota(jnp.int32, regimes)[None, :]
    select = owner_mask.astype(jnp.float32)
    line_re = jnp.einsum("lr,rkj->lkj", select, kern_re, precision=HIGHEST_PRECISION)
    line_im = jnp.einsum("lr,rkj->lkj", select, kern_im, precision=HIGHEST_PRECISION)
    generator_matrix = generator(rate_table, rate_index)
    scale_diff = diffusion[:, None, None]
    scale_jump = jump_rate[:, None, None]
    field = density
    sums = []
    for sweep_index in range(SWEEPS):
        line_data = lax.all_to_all(
            field.reshape(regimes * y_rows, x_cols), "gx", split_axis=0, concat_axis=1, tiled=True
        )
        spec_re, spec_im = forward_lines(line_data, tables)
        prod_re = spec_re * line_re - spec_im * line_im
        prod_im = spec_re * line_im + spec_im * line_re
        jump_line = inverse_lines(prod_re, prod_im, tables)
        mixing = jnp.einsum("rs,ryx->syx", generator_matrix, field, precision=HIGHEST_PRECISION)
        jumped = lax.all_to_all(jump_line, "gx", split_axis=1, concat_axis=0, tiled=True).reshape(
            regimes, y_rows, x_cols
        )
        beside_all = with_halo(
            jnp.stack([field, drift[0][None] * field, drift[1][None] * field]),
            (("gx", 3), ("gy", 2)),
            1,
        )
        field_pad = beside_all[0]
        laplace = (
            field_pad[:, 1:-1, 2:]
            + field_pad[:, 1:-1, :-2]
            + field_pad[:, 2:, 1:-1]
            + field_pad[:, :-2, 1:-1]
            - 4.0 * field
        )
        flow_x = (beside_all[1][:, 1:-1, 2:] - beside_all[1][:, 1:-1, :-2]) * 0.5
        flow_y = (beside_all[2][:, 2:, 1:-1] - beside_all[2][:, :-2, 1:-1]) * 0.5
        updated = (
            field
            + scale_diff * laplace
            - flow_x
            - flow_y
            + scale_jump * (jumped - field)
            - kill[None] * field
            + mixing
        )
        sums.append(jnp.sum(updated))
        field = updated
    cell_count = field.size * lax.axis_size("gx") * lax.axis_size("gy")
    totals = tree_sum(jnp.broadcast_to(jnp.stack(sums)[:, None], (len(sums), 128)))[:, 0]
    scale = jnp.float32(1.0)
    for sweep_index in range(SWEEPS):
        mass_mean = totals[sweep_index] / scale / cell_count
        if sweep_index == SWEEPS - 1:
            field = field / scale / mass_mean
        scale = scale * mass_mean
    return field


def solution(mesh):
    return jax.shard_map(
        local,
        mesh=mesh,
        in_specs=(
            P(None, "gy", "gx"),
            P(None, "gy", "gx"),
            P("gy", "gx"),
            P(),
            P(),
            P(),
            P(),
            P(),
            P(),
        ),
        out_specs=P(None, "gy", "gx"),
        check_vma=False,
    )
```

```python
import math

import jax
import jax.numpy as jnp
from jax import lax
from jax.sharding import PartitionSpec as P

SWEEPS = 2


HIGHEST_PRECISION = lax.Precision.HIGHEST


def with_halo(array, sides, width):
    for axis, dim in sides:
        peers, length = (lax.axis_size(axis), array.shape[dim])
        up = [(i, (i + 1) % peers) for i in range(peers)]
        down = [(j, i) for i, j in up]
        last = lax.slice_in_dim(array, length - width, length, axis=dim)
        leading = lax.slice_in_dim(array, 0, width, axis=dim)
        before = lax.ppermute(last, axis, up)
        after = lax.ppermute(leading, axis, down)
        array = jnp.concatenate([before, array, after], axis=dim)
    return array


def angle_table(height, breadth, period):
    product = (
        lax.broadcasted_iota(jnp.int32, (height, breadth), 0)
        * lax.broadcasted_iota(jnp.int32, (height, breadth), 1)
        % period
    )
    angles = product.astype(jnp.float32) * (2.0 * math.pi / period)
    return (jnp.cos(angles), jnp.sin(angles))


def factor_pair(length):
    low_factor = 1
    factor = 1
    while factor * factor <= length:
        if length % factor == 0:
            low_factor = factor
        factor += 1
    return (low_factor, length // low_factor)


def forward_lines(line_data, tables):
    (cos_a, sin_a), (cos_b, sin_b), (cos_t, sin_t) = tables
    width_a = cos_a.shape[0]
    width_b = cos_b.shape[0]
    line_count = line_data.shape[0]
    blocks = line_data.reshape(line_count, width_a, width_b)
    first_re = jnp.einsum("mab,ak->mkb", blocks, cos_a, precision=HIGHEST_PRECISION)
    first_im = -jnp.einsum("mab,ak->mkb", blocks, sin_a, precision=HIGHEST_PRECISION)
    turned_re = first_re * cos_t + first_im * sin_t
    turned_im = first_im * cos_t - first_re * sin_t
    final_re = jnp.einsum(
        "mkb,bj->mkj", turned_re, cos_b, precision=HIGHEST_PRECISION
    ) + jnp.einsum("mkb,bj->mkj", turned_im, sin_b, precision=HIGHEST_PRECISION)
    final_im = jnp.einsum(
        "mkb,bj->mkj", turned_im, cos_b, precision=HIGHEST_PRECISION
    ) - jnp.einsum("mkb,bj->mkj", turned_re, sin_b, precision=HIGHEST_PRECISION)
    return (final_re, final_im)


def inverse_lines(spec_re, spec_im, tables):
    (cos_a, sin_a), (cos_b, sin_b), (cos_t, sin_t) = tables
    line_count, width_a, width_b = spec_re.shape
    back_re = jnp.einsum("mkj,jb->mkb", spec_re, cos_b, precision=HIGHEST_PRECISION) - jnp.einsum(
        "mkj,jb->mkb", spec_im, sin_b, precision=HIGHEST_PRECISION
    )
    back_im = jnp.einsum("mkj,jb->mkb", spec_re, sin_b, precision=HIGHEST_PRECISION) + jnp.einsum(
        "mkj,jb->mkb", spec_im, cos_b, precision=HIGHEST_PRECISION
    )
    turned_re = back_re * cos_t - back_im * sin_t
    turned_im = back_re * sin_t + back_im * cos_t
    result = jnp.einsum("mkb,ka->mab", turned_re, cos_a, precision=HIGHEST_PRECISION) - jnp.einsum(
        "mkb,ka->mab", turned_im, sin_a, precision=HIGHEST_PRECISION
    )
    return result.reshape(line_count, width_a * width_b) / (width_a * width_b)


def generator(rate_table, rate_index):
    regimes = rate_index.shape[0]
    entries = rate_table.shape[0]
    picked = (rate_index[:, :, None] == lax.iota(jnp.int32, entries)[None, None, :]).astype(
        jnp.float32
    )
    offdiag = jnp.sum(picked * rate_table[None, None, :], axis=2) * (
        1.0 - jnp.eye(regimes, dtype=jnp.float32)
    )
    return offdiag - jnp.diag(jnp.sum(offdiag, axis=1))


def tree_sum(values):
    for axis in ("gx", "gy"):
        peers = lax.axis_size(axis)
        step = 1
        while step < peers:
            pairs = [(i, i ^ step) for i in range(peers)]
            values = values + lax.ppermute(values, axis, pairs)
            step *= 2
    return values


def local(
    density, drift, kill, diffusion, jump_rate, kernel_vals, jump_len, rate_table, rate_index
):
    regimes, y_rows, x_cols = density.shape
    groups = lax.axis_size("gx")
    length = x_cols * groups
    per_dev = regimes * y_rows // groups
    width_a, width_b = factor_pair(length)
    tables = (
        angle_table(width_a, width_a, width_a),
        angle_table(width_b, width_b, width_b),
        angle_table(width_a, width_b, length),
    )
    support = kernel_vals.shape[1]
    inside = lax.broadcasted_iota(jnp.int32, (regimes, support), 1) < jump_len[:, None]
    weights = jnp.where(inside, kernel_vals, jnp.zeros_like(kernel_vals))
    weights = weights / jnp.sum(weights, axis=1, keepdims=True)
    padded = jnp.concatenate(
        [
            jnp.zeros((regimes, 1), jnp.float32),
            weights,
            jnp.zeros((regimes, length - support - 1), jnp.float32),
        ],
        axis=1,
    )
    first_line = lax.axis_index("gx") * per_dev
    if y_rows % per_dev == 0:
        own = lax.dynamic_slice_in_dim(padded, first_line // y_rows, 1, axis=0)
        own_re, own_im = forward_lines(own, tables)
        line_re = jnp.broadcast_to(own_re, (per_dev,) + own_re.shape[1:])
        line_im = jnp.broadcast_to(own_im, (per_dev,) + own_im.shape[1:])
    else:
        kern_re, kern_im = forward_lines(padded, tables)
        line_ids = first_line + lax.iota(jnp.int32, per_dev)
        owner_mask = (line_ids // y_rows)[:, None] == lax.iota(jnp.int32, regimes)[None, :]
        select = owner_mask.astype(jnp.float32)
        line_re = jnp.einsum("lr,rkj->lkj", select, kern_re, precision=HIGHEST_PRECISION)
        line_im = jnp.einsum("lr,rkj->lkj", select, kern_im, precision=HIGHEST_PRECISION)
    generator_matrix = generator(rate_table, rate_index)
    scale_diff = diffusion[:, None, None]
    scale_jump = jump_rate[:, None, None]
    field = density
    sums = []
    for sweep_index in range(SWEEPS):
        line_data = lax.all_to_all(
            field.reshape(regimes * y_rows, x_cols), "gx", split_axis=0, concat_axis=1, tiled=True
        )
        spec_re, spec_im = forward_lines(line_data, tables)
        prod_re = spec_re * line_re - spec_im * line_im
        prod_im = spec_re * line_im + spec_im * line_re
        jump_line = inverse_lines(prod_re, prod_im, tables)
        mixing = jnp.einsum("rs,ryx->syx", generator_matrix, field, precision=HIGHEST_PRECISION)
        jumped = lax.all_to_all(jump_line, "gx", split_axis=1, concat_axis=0, tiled=True).reshape(
            regimes, y_rows, x_cols
        )
        beside_all = with_halo(
            jnp.stack([field, drift[0][None] * field, drift[1][None] * field]),
            (("gx", 3), ("gy", 2)),
            1,
        )
        field_pad = beside_all[0]
        laplace = (
            field_pad[:, 1:-1, 2:]
            + field_pad[:, 1:-1, :-2]
            + field_pad[:, 2:, 1:-1]
            + field_pad[:, :-2, 1:-1]
            - 4.0 * field
        )
        flow_x = (beside_all[1][:, 1:-1, 2:] - beside_all[1][:, 1:-1, :-2]) * 0.5
        flow_y = (beside_all[2][:, 2:, 1:-1] - beside_all[2][:, :-2, 1:-1]) * 0.5
        updated = (
            field
            + scale_diff * laplace
            - flow_x
            - flow_y
            + scale_jump * (jumped - field)
            - kill[None] * field
            + mixing
        )
        sums.append(jnp.sum(updated))
        field = updated
    cell_count = field.size * lax.axis_size("gx") * lax.axis_size("gy")
    totals = tree_sum(jnp.broadcast_to(jnp.stack(sums)[:, None], (len(sums), 128)))[:, 0]
    scale = jnp.float32(1.0)
    for sweep_index in range(SWEEPS):
        mass_mean = totals[sweep_index] / scale / cell_count
        if sweep_index == SWEEPS - 1:
            field = field / scale / mass_mean
        scale = scale * mass_mean
    return field


def solution(mesh):
    return jax.shard_map(
        local,
        mesh=mesh,
        in_specs=(
            P(None, "gy", "gx"),
            P(None, "gy", "gx"),
            P("gy", "gx"),
            P(),
            P(),
            P(),
            P(),
            P(),
            P(),
        ),
        out_specs=P(None, "gy", "gx"),
        check_vma=False,
    )
```

```python
import math

import jax
import jax.numpy as jnp
from jax import lax
from jax.experimental import pallas as pl
from jax.experimental.pallas import tpu as pltpu
from jax.sharding import PartitionSpec as P

SWEEPS = 2


HIGHEST_PRECISION = lax.Precision.HIGHEST


def with_halo(array, sides, width):
    for axis, dim in sides:
        peers, length = (lax.axis_size(axis), array.shape[dim])
        up = [(i, (i + 1) % peers) for i in range(peers)]
        down = [(j, i) for i, j in up]
        last = lax.slice_in_dim(array, length - width, length, axis=dim)
        leading = lax.slice_in_dim(array, 0, width, axis=dim)
        before = lax.ppermute(last, axis, up)
        after = lax.ppermute(leading, axis, down)
        array = jnp.concatenate([before, array, after], axis=dim)
    return array


def angle_table(height, breadth, period):
    product = (
        lax.broadcasted_iota(jnp.int32, (height, breadth), 0)
        * lax.broadcasted_iota(jnp.int32, (height, breadth), 1)
        % period
    )
    angles = product.astype(jnp.float32) * (2.0 * math.pi / period)
    return (jnp.cos(angles), jnp.sin(angles))


def factor_pair(length):
    low_factor = 1
    factor = 1
    while factor * factor <= length:
        if length % factor == 0:
            low_factor = factor
        factor += 1
    return (low_factor, length // low_factor)


def forward_lines(line_data, tables):
    (cos_a, sin_a), (cos_b, sin_b), (cos_t, sin_t) = tables
    width_a = cos_a.shape[0]
    width_b = cos_b.shape[0]
    line_count = line_data.shape[0]
    blocks = line_data.reshape(line_count, width_a, width_b)
    first_re = jnp.einsum("mab,ak->mkb", blocks, cos_a, precision=HIGHEST_PRECISION)
    first_im = -jnp.einsum("mab,ak->mkb", blocks, sin_a, precision=HIGHEST_PRECISION)
    turned_re = first_re * cos_t + first_im * sin_t
    turned_im = first_im * cos_t - first_re * sin_t
    final_re = jnp.einsum(
        "mkb,bj->mkj", turned_re, cos_b, precision=HIGHEST_PRECISION
    ) + jnp.einsum("mkb,bj->mkj", turned_im, sin_b, precision=HIGHEST_PRECISION)
    final_im = jnp.einsum(
        "mkb,bj->mkj", turned_im, cos_b, precision=HIGHEST_PRECISION
    ) - jnp.einsum("mkb,bj->mkj", turned_re, sin_b, precision=HIGHEST_PRECISION)
    return (final_re, final_im)


def inverse_lines(spec_re, spec_im, tables):
    (cos_a, sin_a), (cos_b, sin_b), (cos_t, sin_t) = tables
    line_count, width_a, width_b = spec_re.shape
    back_re = jnp.einsum("mkj,jb->mkb", spec_re, cos_b, precision=HIGHEST_PRECISION) - jnp.einsum(
        "mkj,jb->mkb", spec_im, sin_b, precision=HIGHEST_PRECISION
    )
    back_im = jnp.einsum("mkj,jb->mkb", spec_re, sin_b, precision=HIGHEST_PRECISION) + jnp.einsum(
        "mkj,jb->mkb", spec_im, cos_b, precision=HIGHEST_PRECISION
    )
    turned_re = back_re * cos_t - back_im * sin_t
    turned_im = back_re * sin_t + back_im * cos_t
    result = jnp.einsum("mkb,ka->mab", turned_re, cos_a, precision=HIGHEST_PRECISION) - jnp.einsum(
        "mkb,ka->mab", turned_im, sin_a, precision=HIGHEST_PRECISION
    )
    return result.reshape(line_count, width_a * width_b) / (width_a * width_b)


def generator(rate_table, rate_index):
    regimes = rate_index.shape[0]
    entries = rate_table.shape[0]
    picked = (rate_index[:, :, None] == lax.iota(jnp.int32, entries)[None, None, :]).astype(
        jnp.float32
    )
    offdiag = jnp.sum(picked * rate_table[None, None, :], axis=2) * (
        1.0 - jnp.eye(regimes, dtype=jnp.float32)
    )
    return offdiag - jnp.diag(jnp.sum(offdiag, axis=1))


def exchange_kernel(x_ref, o_ref, buf, send_sems, recv_sems, init_sem):
    gx, gy = lax.axis_index("gx"), lax.axis_index("gy")
    nx, ny = lax.axis_size("gx"), lax.axis_size("gy")
    me = gx * ny + gy
    partners = []
    stride = 1
    while stride < ny:
        bit = (gy // stride) % 2
        partners.append((gx, gy + stride - 2 * stride * bit))
        stride *= 2
    stride = 1
    while stride < nx:
        bit = (gx // stride) % 2
        partners.append((gx + stride - 2 * stride * bit, gy))
        stride *= 2
    barrier = pltpu.get_barrier_semaphore()
    for peer in partners:
        pl.semaphore_signal(barrier, 1, device_id=peer, device_id_type=pl.DeviceIdType.MESH)
    pl.semaphore_wait(barrier, len(partners))
    own = pltpu.make_async_copy(x_ref, buf.at[pl.ds(me, 1)], init_sem)
    own.start()
    own.wait()
    for stage, peer in enumerate(partners):
        size = 1 << stage
        start = (me // size) * size
        block = buf.at[pl.ds(start, size)]
        copy = pltpu.make_async_remote_copy(
            src_ref=block,
            dst_ref=block,
            send_sem=send_sems.at[stage],
            recv_sem=recv_sems.at[stage],
            device_id=peer,
            device_id_type=pl.DeviceIdType.MESH,
        )
        copy.start()
        copy.wait()
    o_ref[...] = jnp.sum(buf[...], axis=0)


def tree_sum(values):
    count = values.shape[0]
    peers = lax.axis_size("gx") * lax.axis_size("gy")
    stages = peers.bit_length() - 1
    slab = jnp.pad(values[None, :], ((0, 7), (0, 128 - count)))[None]
    total = pl.pallas_call(
        exchange_kernel,
        out_shape=jax.ShapeDtypeStruct((8, 128), jnp.float32),
        in_specs=[pl.BlockSpec(memory_space=pltpu.VMEM)],
        out_specs=pl.BlockSpec(memory_space=pltpu.VMEM),
        scratch_shapes=[
            pltpu.VMEM((peers, 8, 128), jnp.float32),
            pltpu.SemaphoreType.DMA((stages,)),
            pltpu.SemaphoreType.DMA((stages,)),
            pltpu.SemaphoreType.DMA,
        ],
        compiler_params=pltpu.CompilerParams(collective_id=0, has_side_effects=True),
    )(slab)
    return total[0, :count]


def local(
    density, drift, kill, diffusion, jump_rate, kernel_vals, jump_len, rate_table, rate_index
):
    regimes, y_rows, x_cols = density.shape
    groups = lax.axis_size("gx")
    length = x_cols * groups
    per_dev = regimes * y_rows // groups
    width_a, width_b = factor_pair(length)
    tables = (
        angle_table(width_a, width_a, width_a),
        angle_table(width_b, width_b, width_b),
        angle_table(width_a, width_b, length),
    )
    support = kernel_vals.shape[1]
    inside = lax.broadcasted_iota(jnp.int32, (regimes, support), 1) < jump_len[:, None]
    weights = jnp.where(inside, kernel_vals, jnp.zeros_like(kernel_vals))
    weights = weights / jnp.sum(weights, axis=1, keepdims=True)
    padded = jnp.concatenate(
        [
            jnp.zeros((regimes, 1), jnp.float32),
            weights,
            jnp.zeros((regimes, length - support - 1), jnp.float32),
        ],
        axis=1,
    )
    first_line = lax.axis_index("gx") * per_dev
    if y_rows % per_dev == 0:
        own = lax.dynamic_slice_in_dim(padded, first_line // y_rows, 1, axis=0)
        own_re, own_im = forward_lines(own, tables)
        line_re = jnp.broadcast_to(own_re, (per_dev,) + own_re.shape[1:])
        line_im = jnp.broadcast_to(own_im, (per_dev,) + own_im.shape[1:])
    else:
        kern_re, kern_im = forward_lines(padded, tables)
        line_ids = first_line + lax.iota(jnp.int32, per_dev)
        owner_mask = (line_ids // y_rows)[:, None] == lax.iota(jnp.int32, regimes)[None, :]
        select = owner_mask.astype(jnp.float32)
        line_re = jnp.einsum("lr,rkj->lkj", select, kern_re, precision=HIGHEST_PRECISION)
        line_im = jnp.einsum("lr,rkj->lkj", select, kern_im, precision=HIGHEST_PRECISION)
    generator_matrix = generator(rate_table, rate_index)
    scale_diff = diffusion[:, None, None]
    scale_jump = jump_rate[:, None, None]
    field = density
    sums = []
    for sweep_index in range(SWEEPS):
        line_data = lax.all_to_all(
            field.reshape(regimes * y_rows, x_cols), "gx", split_axis=0, concat_axis=1, tiled=True
        )
        spec_re, spec_im = forward_lines(line_data, tables)
        prod_re = spec_re * line_re - spec_im * line_im
        prod_im = spec_re * line_im + spec_im * line_re
        jump_line = inverse_lines(prod_re, prod_im, tables)
        mixing = jnp.einsum("rs,ryx->syx", generator_matrix, field, precision=HIGHEST_PRECISION)
        jumped = lax.all_to_all(jump_line, "gx", split_axis=1, concat_axis=0, tiled=True).reshape(
            regimes, y_rows, x_cols
        )
        beside_all = with_halo(
            jnp.stack([field, drift[0][None] * field, drift[1][None] * field]),
            (("gx", 3), ("gy", 2)),
            1,
        )
        field_pad = beside_all[0]
        laplace = (
            field_pad[:, 1:-1, 2:]
            + field_pad[:, 1:-1, :-2]
            + field_pad[:, 2:, 1:-1]
            + field_pad[:, :-2, 1:-1]
            - 4.0 * field
        )
        flow_x = (beside_all[1][:, 1:-1, 2:] - beside_all[1][:, 1:-1, :-2]) * 0.5
        flow_y = (beside_all[2][:, 2:, 1:-1] - beside_all[2][:, :-2, 1:-1]) * 0.5
        updated = (
            field
            + scale_diff * laplace
            - flow_x
            - flow_y
            + scale_jump * (jumped - field)
            - kill[None] * field
            + mixing
        )
        sums.append(jnp.sum(updated))
        field = updated
    cell_count = field.size * lax.axis_size("gx") * lax.axis_size("gy")
    totals = tree_sum(jnp.stack(sums))
    scale = jnp.float32(1.0)
    for sweep_index in range(SWEEPS):
        mass_mean = totals[sweep_index] / scale / cell_count
        if sweep_index == SWEEPS - 1:
            field = field / scale / mass_mean
        scale = scale * mass_mean
    return field


def solution(mesh):
    return jax.shard_map(
        local,
        mesh=mesh,
        in_specs=(
            P(None, "gy", "gx"),
            P(None, "gy", "gx"),
            P("gy", "gx"),
            P(),
            P(),
            P(),
            P(),
            P(),
            P(),
        ),
        out_specs=P(None, "gy", "gx"),
        check_vma=False,
    )
```

```python
import math

import jax
import jax.numpy as jnp
from jax import lax
from jax.sharding import PartitionSpec as P

SWEEPS = 2


HIGHEST_PRECISION = lax.Precision.HIGH


def with_halo(array, sides, width):
    for axis, dim in sides:
        peers, length = (lax.axis_size(axis), array.shape[dim])
        up = [(i, (i + 1) % peers) for i in range(peers)]
        down = [(j, i) for i, j in up]
        last = lax.slice_in_dim(array, length - width, length, axis=dim)
        leading = lax.slice_in_dim(array, 0, width, axis=dim)
        before = lax.ppermute(last, axis, up)
        after = lax.ppermute(leading, axis, down)
        array = jnp.concatenate([before, array, after], axis=dim)
    return array


def angle_table(height, breadth, period):
    product = (
        lax.broadcasted_iota(jnp.int32, (height, breadth), 0)
        * lax.broadcasted_iota(jnp.int32, (height, breadth), 1)
        % period
    )
    angles = product.astype(jnp.float32) * (2.0 * math.pi / period)
    return (jnp.cos(angles), jnp.sin(angles))


def factor_pair(length):
    low_factor = 1
    factor = 1
    while factor * factor <= length:
        if length % factor == 0:
            low_factor = factor
        factor += 1
    return (low_factor, length // low_factor)


def forward_lines(line_data, tables):
    (cos_a, sin_a), (cos_b, sin_b), (cos_t, sin_t) = tables
    width_a = cos_a.shape[0]
    width_b = cos_b.shape[0]
    line_count = line_data.shape[0]
    blocks = line_data.reshape(line_count, width_a, width_b)
    first_re = jnp.einsum("mab,ak->mkb", blocks, cos_a, precision=HIGHEST_PRECISION)
    first_im = -jnp.einsum("mab,ak->mkb", blocks, sin_a, precision=HIGHEST_PRECISION)
    turned_re = first_re * cos_t + first_im * sin_t
    turned_im = first_im * cos_t - first_re * sin_t
    final_re = jnp.einsum(
        "mkb,bj->mkj", turned_re, cos_b, precision=HIGHEST_PRECISION
    ) + jnp.einsum("mkb,bj->mkj", turned_im, sin_b, precision=HIGHEST_PRECISION)
    final_im = jnp.einsum(
        "mkb,bj->mkj", turned_im, cos_b, precision=HIGHEST_PRECISION
    ) - jnp.einsum("mkb,bj->mkj", turned_re, sin_b, precision=HIGHEST_PRECISION)
    return (final_re, final_im)


def inverse_lines(spec_re, spec_im, tables):
    (cos_a, sin_a), (cos_b, sin_b), (cos_t, sin_t) = tables
    line_count, width_a, width_b = spec_re.shape
    back_re = jnp.einsum("mkj,jb->mkb", spec_re, cos_b, precision=HIGHEST_PRECISION) - jnp.einsum(
        "mkj,jb->mkb", spec_im, sin_b, precision=HIGHEST_PRECISION
    )
    back_im = jnp.einsum("mkj,jb->mkb", spec_re, sin_b, precision=HIGHEST_PRECISION) + jnp.einsum(
        "mkj,jb->mkb", spec_im, cos_b, precision=HIGHEST_PRECISION
    )
    turned_re = back_re * cos_t - back_im * sin_t
    turned_im = back_re * sin_t + back_im * cos_t
    result = jnp.einsum("mkb,ka->mab", turned_re, cos_a, precision=HIGHEST_PRECISION) - jnp.einsum(
        "mkb,ka->mab", turned_im, sin_a, precision=HIGHEST_PRECISION
    )
    return result.reshape(line_count, width_a * width_b) / (width_a * width_b)


def generator(rate_table, rate_index):
    regimes = rate_index.shape[0]
    entries = rate_table.shape[0]
    picked = (rate_index[:, :, None] == lax.iota(jnp.int32, entries)[None, None, :]).astype(
        jnp.float32
    )
    offdiag = jnp.sum(picked * rate_table[None, None, :], axis=2) * (
        1.0 - jnp.eye(regimes, dtype=jnp.float32)
    )
    return offdiag - jnp.diag(jnp.sum(offdiag, axis=1))


def tree_sum(values):
    for axis in ("gx", "gy"):
        peers = lax.axis_size(axis)
        step = 1
        while step < peers:
            pairs = [(i, i ^ step) for i in range(peers)]
            values = values + lax.ppermute(values, axis, pairs)
            step *= 2
    return values


def local(
    density, drift, kill, diffusion, jump_rate, kernel_vals, jump_len, rate_table, rate_index
):
    regimes, y_rows, x_cols = density.shape
    groups = lax.axis_size("gx")
    length = x_cols * groups
    per_dev = regimes * y_rows // groups
    width_a, width_b = factor_pair(length)
    tables = (
        angle_table(width_a, width_a, width_a),
        angle_table(width_b, width_b, width_b),
        angle_table(width_a, width_b, length),
    )
    support = kernel_vals.shape[1]
    inside = lax.broadcasted_iota(jnp.int32, (regimes, support), 1) < jump_len[:, None]
    weights = jnp.where(inside, kernel_vals, jnp.zeros_like(kernel_vals))
    weights = weights / jnp.sum(weights, axis=1, keepdims=True)
    padded = jnp.concatenate(
        [
            jnp.zeros((regimes, 1), jnp.float32),
            weights,
            jnp.zeros((regimes, length - support - 1), jnp.float32),
        ],
        axis=1,
    )
    first_line = lax.axis_index("gx") * per_dev
    if y_rows % per_dev == 0:
        own = lax.dynamic_slice_in_dim(padded, first_line // y_rows, 1, axis=0)
        own_re, own_im = forward_lines(own, tables)
        line_re = jnp.broadcast_to(own_re, (per_dev,) + own_re.shape[1:])
        line_im = jnp.broadcast_to(own_im, (per_dev,) + own_im.shape[1:])
    else:
        kern_re, kern_im = forward_lines(padded, tables)
        line_ids = first_line + lax.iota(jnp.int32, per_dev)
        owner_mask = (line_ids // y_rows)[:, None] == lax.iota(jnp.int32, regimes)[None, :]
        select = owner_mask.astype(jnp.float32)
        line_re = jnp.einsum("lr,rkj->lkj", select, kern_re, precision=HIGHEST_PRECISION)
        line_im = jnp.einsum("lr,rkj->lkj", select, kern_im, precision=HIGHEST_PRECISION)
    generator_matrix = generator(rate_table, rate_index)
    scale_diff = diffusion[:, None, None]
    scale_jump = jump_rate[:, None, None]
    field = density
    sums = []
    for sweep_index in range(SWEEPS):
        line_data = lax.all_to_all(
            field.reshape(regimes * y_rows, x_cols), "gx", split_axis=0, concat_axis=1, tiled=True
        )
        spec_re, spec_im = forward_lines(line_data, tables)
        prod_re = spec_re * line_re - spec_im * line_im
        prod_im = spec_re * line_im + spec_im * line_re
        jump_line = inverse_lines(prod_re, prod_im, tables)
        mixing = jnp.einsum("rs,ryx->syx", generator_matrix, field, precision=HIGHEST_PRECISION)
        jumped = lax.all_to_all(jump_line, "gx", split_axis=1, concat_axis=0, tiled=True).reshape(
            regimes, y_rows, x_cols
        )
        beside_all = with_halo(
            jnp.stack([field, drift[0][None] * field, drift[1][None] * field]),
            (("gx", 3), ("gy", 2)),
            1,
        )
        field_pad = beside_all[0]
        laplace = (
            field_pad[:, 1:-1, 2:]
            + field_pad[:, 1:-1, :-2]
            + field_pad[:, 2:, 1:-1]
            + field_pad[:, :-2, 1:-1]
            - 4.0 * field
        )
        flow_x = (beside_all[1][:, 1:-1, 2:] - beside_all[1][:, 1:-1, :-2]) * 0.5
        flow_y = (beside_all[2][:, 2:, 1:-1] - beside_all[2][:, :-2, 1:-1]) * 0.5
        updated = (
            field
            + scale_diff * laplace
            - flow_x
            - flow_y
            + scale_jump * (jumped - field)
            - kill[None] * field
            + mixing
        )
        sums.append(jnp.sum(updated))
        field = updated
    cell_count = field.size * lax.axis_size("gx") * lax.axis_size("gy")
    totals = tree_sum(jnp.broadcast_to(jnp.stack(sums)[:, None], (len(sums), 128)))[:, 0]
    scale = jnp.float32(1.0)
    for sweep_index in range(SWEEPS):
        mass_mean = totals[sweep_index] / scale / cell_count
        if sweep_index == SWEEPS - 1:
            field = field / scale / mass_mean
        scale = scale * mass_mean
    return field


def solution(mesh):
    return jax.shard_map(
        local,
        mesh=mesh,
        in_specs=(
            P(None, "gy", "gx"),
            P(None, "gy", "gx"),
            P("gy", "gx"),
            P(),
            P(),
            P(),
            P(),
            P(),
            P(),
        ),
        out_specs=P(None, "gy", "gx"),
        check_vma=False,
    )
```

```python
import math

import jax
import jax.numpy as jnp
from jax import lax
from jax.sharding import PartitionSpec as P

SWEEPS = 2


HIGHEST_PRECISION = lax.Precision.HIGH


def with_halo(array, sides, width):
    for axis, dim in sides:
        peers, length = (lax.axis_size(axis), array.shape[dim])
        up = [(i, (i + 1) % peers) for i in range(peers)]
        down = [(j, i) for i, j in up]
        last = lax.slice_in_dim(array, length - width, length, axis=dim)
        leading = lax.slice_in_dim(array, 0, width, axis=dim)
        before = lax.ppermute(last, axis, up)
        after = lax.ppermute(leading, axis, down)
        array = jnp.concatenate([before, array, after], axis=dim)
    return array


def angle_table(height, breadth, period):
    product = (
        lax.broadcasted_iota(jnp.int32, (height, breadth), 0)
        * lax.broadcasted_iota(jnp.int32, (height, breadth), 1)
        % period
    )
    angles = product.astype(jnp.float32) * (2.0 * math.pi / period)
    return (jnp.cos(angles), jnp.sin(angles))


def factor_pair(length):
    low_factor = 1
    factor = 1
    while factor * factor <= length:
        if length % factor == 0:
            low_factor = factor
        factor += 1
    return (low_factor, length // low_factor)


def forward_lines(line_data, tables):
    (cos_a, sin_a), (cos_b, sin_b), (cos_t, sin_t) = tables
    width_a = cos_a.shape[0]
    width_b = cos_b.shape[0]
    line_count = line_data.shape[0]
    blocks = line_data.reshape(line_count, width_a, width_b)
    table_a = jnp.concatenate([cos_a, -sin_a], axis=1)
    first = jnp.einsum("mab,ak->mkb", blocks, table_a, precision=HIGHEST_PRECISION)
    first_re, first_im = first[:, :width_a], first[:, width_a:]
    turned_re = first_re * cos_t + first_im * sin_t
    turned_im = first_im * cos_t - first_re * sin_t
    table_b = jnp.concatenate(
        [jnp.concatenate([cos_b, -sin_b], axis=1), jnp.concatenate([sin_b, cos_b], axis=1)], axis=0
    )
    turned = jnp.concatenate([turned_re, turned_im], axis=2)
    final = jnp.einsum("mkb,bj->mkj", turned, table_b, precision=HIGHEST_PRECISION)
    return (final[:, :, :width_b], final[:, :, width_b:])


def inverse_lines(spec_re, spec_im, tables):
    (cos_a, sin_a), (cos_b, sin_b), (cos_t, sin_t) = tables
    line_count, width_a, width_b = spec_re.shape
    table_b = jnp.concatenate(
        [jnp.concatenate([cos_b, sin_b], axis=1), jnp.concatenate([-sin_b, cos_b], axis=1)], axis=0
    )
    back = jnp.einsum(
        "mkj,jb->mkb", jnp.concatenate([spec_re, spec_im], axis=2), table_b,
        precision=HIGHEST_PRECISION,
    )
    back_re, back_im = back[:, :, :width_b], back[:, :, width_b:]
    turned_re = back_re * cos_t - back_im * sin_t
    turned_im = back_re * sin_t + back_im * cos_t
    table_a = jnp.concatenate([cos_a, -sin_a], axis=0)
    result = jnp.einsum(
        "mkb,ka->mab", jnp.concatenate([turned_re, turned_im], axis=1), table_a,
        precision=HIGHEST_PRECISION,
    )
    return result.reshape(line_count, width_a * width_b)


def generator(rate_table, rate_index):
    regimes = rate_index.shape[0]
    entries = rate_table.shape[0]
    picked = (rate_index[:, :, None] == lax.iota(jnp.int32, entries)[None, None, :]).astype(
        jnp.float32
    )
    offdiag = jnp.sum(picked * rate_table[None, None, :], axis=2) * (
        1.0 - jnp.eye(regimes, dtype=jnp.float32)
    )
    return offdiag - jnp.diag(jnp.sum(offdiag, axis=1))


def tree_sum(values):
    for axis in ("gx", "gy"):
        peers = lax.axis_size(axis)
        step = 1
        while step < peers:
            pairs = [(i, i ^ step) for i in range(peers)]
            values = values + lax.ppermute(values, axis, pairs)
            step *= 2
    return values


def local(
    density, drift, kill, diffusion, jump_rate, kernel_vals, jump_len, rate_table, rate_index
):
    regimes, y_rows, x_cols = density.shape
    groups = lax.axis_size("gx")
    length = x_cols * groups
    per_dev = regimes * y_rows // groups
    width_a, width_b = factor_pair(length)
    tables = (
        angle_table(width_a, width_a, width_a),
        angle_table(width_b, width_b, width_b),
        angle_table(width_a, width_b, length),
    )
    support = kernel_vals.shape[1]
    inside = lax.broadcasted_iota(jnp.int32, (regimes, support), 1) < jump_len[:, None]
    weights = jnp.where(inside, kernel_vals, jnp.zeros_like(kernel_vals))
    weights = weights / jnp.sum(weights, axis=1, keepdims=True)
    padded = jnp.concatenate(
        [
            jnp.zeros((regimes, 1), jnp.float32),
            weights,
            jnp.zeros((regimes, length - support - 1), jnp.float32),
        ],
        axis=1,
    )
    first_line = lax.axis_index("gx") * per_dev
    if y_rows % per_dev == 0:
        own = lax.dynamic_slice_in_dim(padded, first_line // y_rows, 1, axis=0)
        own_re, own_im = forward_lines(own, tables)
        line_re = jnp.broadcast_to(own_re / length, (per_dev,) + own_re.shape[1:])
        line_im = jnp.broadcast_to(own_im / length, (per_dev,) + own_im.shape[1:])
    else:
        kern_re, kern_im = forward_lines(padded, tables)
        line_ids = first_line + lax.iota(jnp.int32, per_dev)
        owner_mask = (line_ids // y_rows)[:, None] == lax.iota(jnp.int32, regimes)[None, :]
        select = owner_mask.astype(jnp.float32)
        line_re = jnp.einsum("lr,rkj->lkj", select, kern_re / length, precision=HIGHEST_PRECISION)
        line_im = jnp.einsum("lr,rkj->lkj", select, kern_im / length, precision=HIGHEST_PRECISION)
    generator_matrix = generator(rate_table, rate_index)
    scale_diff = diffusion[:, None, None]
    scale_jump = jump_rate[:, None, None]
    field = density
    sums = []
    for sweep_index in range(SWEEPS):
        line_data = lax.all_to_all(
            field.reshape(regimes * y_rows, x_cols), "gx", split_axis=0, concat_axis=1, tiled=True
        )
        spec_re, spec_im = forward_lines(line_data, tables)
        prod_re = spec_re * line_re - spec_im * line_im
        prod_im = spec_re * line_im + spec_im * line_re
        jump_line = inverse_lines(prod_re, prod_im, tables)
        mixing = jnp.einsum("rs,ryx->syx", generator_matrix, field, precision=HIGHEST_PRECISION)
        jumped = lax.all_to_all(jump_line, "gx", split_axis=1, concat_axis=0, tiled=True).reshape(
            regimes, y_rows, x_cols
        )
        beside_all = with_halo(
            jnp.stack([field, drift[0][None] * field, drift[1][None] * field]),
            (("gx", 3), ("gy", 2)),
            1,
        )
        field_pad = beside_all[0]
        laplace = (
            field_pad[:, 1:-1, 2:]
            + field_pad[:, 1:-1, :-2]
            + field_pad[:, 2:, 1:-1]
            + field_pad[:, :-2, 1:-1]
            - 4.0 * field
        )
        flow_x = (beside_all[1][:, 1:-1, 2:] - beside_all[1][:, 1:-1, :-2]) * 0.5
        flow_y = (beside_all[2][:, 2:, 1:-1] - beside_all[2][:, :-2, 1:-1]) * 0.5
        updated = (
            field
            + scale_diff * laplace
            - flow_x
            - flow_y
            + scale_jump * (jumped - field)
            - kill[None] * field
            + mixing
        )
        sums.append(jnp.sum(updated))
        field = updated
    cell_count = field.size * lax.axis_size("gx") * lax.axis_size("gy")
    totals = tree_sum(jnp.broadcast_to(jnp.stack(sums)[:, None], (len(sums), 128)))[:, 0]
    scale = jnp.float32(1.0)
    for sweep_index in range(SWEEPS):
        mass_mean = totals[sweep_index] / scale / cell_count
        if sweep_index == SWEEPS - 1:
            field = field / scale / mass_mean
        scale = scale * mass_mean
    return field


def solution(mesh):
    return jax.shard_map(
        local,
        mesh=mesh,
        in_specs=(
            P(None, "gy", "gx"),
            P(None, "gy", "gx"),
            P("gy", "gx"),
            P(),
            P(),
            P(),
            P(),
            P(),
            P(),
        ),
        out_specs=P(None, "gy", "gx"),
        check_vma=False,
    )
```

```python
import math

import jax
import jax.numpy as jnp
from jax import lax
from jax.sharding import PartitionSpec as P

SWEEPS = 2


HIGHEST_PRECISION = lax.Precision.HIGH


def with_halo(array, sides, width):
    for axis, dim in sides:
        peers, length = (lax.axis_size(axis), array.shape[dim])
        up = [(i, (i + 1) % peers) for i in range(peers)]
        down = [(j, i) for i, j in up]
        last = lax.slice_in_dim(array, length - width, length, axis=dim)
        leading = lax.slice_in_dim(array, 0, width, axis=dim)
        before = lax.ppermute(last, axis, up)
        after = lax.ppermute(leading, axis, down)
        array = jnp.concatenate([before, array, after], axis=dim)
    return array


def angle_table(height, breadth, period):
    product = (
        lax.broadcasted_iota(jnp.int32, (height, breadth), 0)
        * lax.broadcasted_iota(jnp.int32, (height, breadth), 1)
        % period
    )
    angles = product.astype(jnp.float32) * (2.0 * math.pi / period)
    return (jnp.cos(angles), jnp.sin(angles))


def factor_pair(length):
    low_factor = 1
    factor = 1
    while factor * factor <= length:
        if length % factor == 0:
            low_factor = factor
        factor += 1
    return (low_factor, length // low_factor)


def forward_lines(line_data, tables):
    (cos_a, sin_a), (cos_b, sin_b), (cos_t, sin_t) = tables
    width_a = cos_a.shape[0]
    width_b = cos_b.shape[0]
    line_count = line_data.shape[0]
    blocks = line_data.reshape(line_count, width_a, width_b)
    table_a = jnp.concatenate([cos_a, -sin_a], axis=1)
    first = jnp.einsum("mab,ak->mkb", blocks, table_a, precision=HIGHEST_PRECISION)
    first_re, first_im = first[:, :width_a], first[:, width_a:]
    turned_re = first_re * cos_t + first_im * sin_t
    turned_im = first_im * cos_t - first_re * sin_t
    table_b = jnp.concatenate(
        [jnp.concatenate([cos_b, -sin_b], axis=1), jnp.concatenate([sin_b, cos_b], axis=1)], axis=0
    )
    turned = jnp.concatenate([turned_re, turned_im], axis=2)
    final = jnp.einsum("mkb,bj->mkj", turned, table_b, precision=HIGHEST_PRECISION)
    return (final[:, :, :width_b], final[:, :, width_b:])


def inverse_lines(spec_re, spec_im, tables):
    (cos_a, sin_a), (cos_b, sin_b), (cos_t, sin_t) = tables
    line_count, width_a, width_b = spec_re.shape
    table_b = jnp.concatenate(
        [jnp.concatenate([cos_b, sin_b], axis=1), jnp.concatenate([-sin_b, cos_b], axis=1)], axis=0
    )
    back = jnp.einsum(
        "mkj,jb->mkb", jnp.concatenate([spec_re, spec_im], axis=2), table_b,
        precision=HIGHEST_PRECISION,
    )
    back_re, back_im = back[:, :, :width_b], back[:, :, width_b:]
    turned_re = back_re * cos_t - back_im * sin_t
    turned_im = back_re * sin_t + back_im * cos_t
    table_a = jnp.concatenate([cos_a, -sin_a], axis=0)
    result = jnp.einsum(
        "mkb,ka->mab", jnp.concatenate([turned_re, turned_im], axis=1), table_a,
        precision=HIGHEST_PRECISION,
    )
    return result.reshape(line_count, width_a * width_b)


def generator(rate_table, rate_index):
    regimes = rate_index.shape[0]
    entries = rate_table.shape[0]
    picked = (rate_index[:, :, None] == lax.iota(jnp.int32, entries)[None, None, :]).astype(
        jnp.float32
    )
    offdiag = jnp.sum(picked * rate_table[None, None, :], axis=2) * (
        1.0 - jnp.eye(regimes, dtype=jnp.float32)
    )
    return offdiag - jnp.diag(jnp.sum(offdiag, axis=1))


def tree_sum(values):
    for axis in ("gx", "gy"):
        peers = lax.axis_size(axis)
        step = 1
        while step < peers:
            pairs = [(i, i ^ step) for i in range(peers)]
            values = values + lax.ppermute(values, axis, pairs)
            step *= 2
    return values


def local(
    density, drift, kill, diffusion, jump_rate, kernel_vals, jump_len, rate_table, rate_index
):
    regimes, y_rows, x_cols = density.shape
    groups = lax.axis_size("gx")
    length = x_cols * groups
    per_dev = regimes * y_rows // groups
    width_a, width_b = factor_pair(length)
    tables = (
        angle_table(width_a, width_a, width_a),
        angle_table(width_b, width_b, width_b),
        angle_table(width_a, width_b, length),
    )
    support = kernel_vals.shape[1]
    inside = lax.broadcasted_iota(jnp.int32, (regimes, support), 1) < jump_len[:, None]
    weights = jnp.where(inside, kernel_vals, jnp.zeros_like(kernel_vals))
    weights = weights / jnp.sum(weights, axis=1, keepdims=True)

    def pad_lines(rows):
        return jnp.pad(rows, ((0, 0), (1, length - support - 1)))

    first_line = lax.axis_index("gx") * per_dev
    if y_rows % per_dev == 0:
        own = pad_lines(lax.dynamic_slice_in_dim(weights, first_line // y_rows, 1, axis=0))
        own_re, own_im = forward_lines(own, tables)
        line_re = jnp.broadcast_to(own_re / length, (per_dev,) + own_re.shape[1:])
        line_im = jnp.broadcast_to(own_im / length, (per_dev,) + own_im.shape[1:])
    else:
        kern_re, kern_im = forward_lines(pad_lines(weights), tables)
        line_ids = first_line + lax.iota(jnp.int32, per_dev)
        owner_mask = (line_ids // y_rows)[:, None] == lax.iota(jnp.int32, regimes)[None, :]
        select = owner_mask.astype(jnp.float32)
        line_re = jnp.einsum("lr,rkj->lkj", select, kern_re / length, precision=HIGHEST_PRECISION)
        line_im = jnp.einsum("lr,rkj->lkj", select, kern_im / length, precision=HIGHEST_PRECISION)
    generator_matrix = generator(rate_table, rate_index)
    scale_diff = diffusion[:, None, None]
    scale_jump = jump_rate[:, None, None]
    field = density
    sums = []
    for sweep_index in range(SWEEPS):
        line_data = lax.all_to_all(
            field.reshape(regimes * y_rows, x_cols), "gx", split_axis=0, concat_axis=1, tiled=True
        )
        spec_re, spec_im = forward_lines(line_data, tables)
        prod_re = spec_re * line_re - spec_im * line_im
        prod_im = spec_re * line_im + spec_im * line_re
        jump_line = inverse_lines(prod_re, prod_im, tables)
        mixing = jnp.einsum("rs,ryx->syx", generator_matrix, field, precision=HIGHEST_PRECISION)
        jumped = lax.all_to_all(jump_line, "gx", split_axis=1, concat_axis=0, tiled=True).reshape(
            regimes, y_rows, x_cols
        )
        beside_x = with_halo(jnp.stack([field, drift[0][None] * field]), (("gx", 3),), 1)
        beside_y = with_halo(jnp.stack([field, drift[1][None] * field]), (("gy", 2),), 1)
        laplace = (
            beside_x[0][:, :, 2:]
            + beside_x[0][:, :, :-2]
            + beside_y[0][:, 2:, :]
            + beside_y[0][:, :-2, :]
            - 4.0 * field
        )
        flow_x = (beside_x[1][:, :, 2:] - beside_x[1][:, :, :-2]) * 0.5
        flow_y = (beside_y[1][:, 2:, :] - beside_y[1][:, :-2, :]) * 0.5
        updated = (
            field
            + scale_diff * laplace
            - flow_x
            - flow_y
            + scale_jump * (jumped - field)
            - kill[None] * field
            + mixing
        )
        sums.append(jnp.sum(updated))
        field = updated
    cell_count = field.size * lax.axis_size("gx") * lax.axis_size("gy")
    totals = tree_sum(jnp.broadcast_to(jnp.stack(sums)[:, None], (len(sums), 128)))[:, 0]
    scale = jnp.float32(1.0)
    for sweep_index in range(SWEEPS):
        mass_mean = totals[sweep_index] / scale / cell_count
        if sweep_index == SWEEPS - 1:
            field = field / scale / mass_mean
        scale = scale * mass_mean
    return field


def solution(mesh):
    return jax.shard_map(
        local,
        mesh=mesh,
        in_specs=(
            P(None, "gy", "gx"),
            P(None, "gy", "gx"),
            P("gy", "gx"),
            P(),
            P(),
            P(),
            P(),
            P(),
            P(),
        ),
        out_specs=P(None, "gy", "gx"),
        check_vma=False,
    )
```

```python
import math

import jax
import jax.numpy as jnp
from jax import lax
from jax.sharding import PartitionSpec as P

SWEEPS = 2


HIGHEST_PRECISION = lax.Precision.HIGH


def with_halo(array, sides, width):
    for axis, dim in sides:
        peers, length = (lax.axis_size(axis), array.shape[dim])
        up = [(i, (i + 1) % peers) for i in range(peers)]
        down = [(j, i) for i, j in up]
        last = lax.slice_in_dim(array, length - width, length, axis=dim)
        leading = lax.slice_in_dim(array, 0, width, axis=dim)
        before = lax.ppermute(last, axis, up)
        after = lax.ppermute(leading, axis, down)
        array = jnp.concatenate([before, array, after], axis=dim)
    return array


def angle_table(height, breadth, period):
    product = (
        lax.broadcasted_iota(jnp.int32, (height, breadth), 0)
        * lax.broadcasted_iota(jnp.int32, (height, breadth), 1)
        % period
    )
    angles = product.astype(jnp.float32) * (2.0 * math.pi / period)
    return (jnp.cos(angles), jnp.sin(angles))


def factor_pair(length):
    low_factor = 1
    factor = 1
    while factor * factor <= length:
        if length % factor == 0:
            low_factor = factor
        factor += 1
    return (low_factor, length // low_factor)


def forward_lines(line_data, tables):
    (cos_a, sin_a), (cos_b, sin_b), (cos_t, sin_t) = tables
    width_a = cos_a.shape[0]
    width_b = cos_b.shape[0]
    line_count = line_data.shape[0]
    blocks = line_data.reshape(line_count, width_a, width_b)
    table_a = jnp.concatenate([cos_a, -sin_a], axis=1)
    first = jnp.einsum("mab,ak->mkb", blocks, table_a, precision=HIGHEST_PRECISION)
    first_re, first_im = first[:, :width_a], first[:, width_a:]
    turned_re = first_re * cos_t + first_im * sin_t
    turned_im = first_im * cos_t - first_re * sin_t
    table_b = jnp.concatenate(
        [jnp.concatenate([cos_b, -sin_b], axis=1), jnp.concatenate([sin_b, cos_b], axis=1)], axis=0
    )
    turned = jnp.concatenate([turned_re, turned_im], axis=2)
    final = jnp.einsum("mkb,bj->mkj", turned, table_b, precision=HIGHEST_PRECISION)
    return (final[:, :, :width_b], final[:, :, width_b:])


def inverse_lines(spec_re, spec_im, tables):
    (cos_a, sin_a), (cos_b, sin_b), (cos_t, sin_t) = tables
    line_count, width_a, width_b = spec_re.shape
    table_b = jnp.concatenate(
        [jnp.concatenate([cos_b, sin_b], axis=1), jnp.concatenate([-sin_b, cos_b], axis=1)], axis=0
    )
    back = jnp.einsum(
        "mkj,jb->mkb", jnp.concatenate([spec_re, spec_im], axis=2), table_b,
        precision=HIGHEST_PRECISION,
    )
    back_re, back_im = back[:, :, :width_b], back[:, :, width_b:]
    turned_re = back_re * cos_t - back_im * sin_t
    turned_im = back_re * sin_t + back_im * cos_t
    table_a = jnp.concatenate([cos_a, -sin_a], axis=0)
    result = jnp.einsum(
        "mkb,ka->mab", jnp.concatenate([turned_re, turned_im], axis=1), table_a,
        precision=HIGHEST_PRECISION,
    )
    return result.reshape(line_count, width_a * width_b)


def generator(rate_table, rate_index):
    regimes = rate_index.shape[0]
    entries = rate_table.shape[0]
    picked = (rate_index[:, :, None] == lax.iota(jnp.int32, entries)[None, None, :]).astype(
        jnp.float32
    )
    offdiag = jnp.sum(picked * rate_table[None, None, :], axis=2) * (
        1.0 - jnp.eye(regimes, dtype=jnp.float32)
    )
    return offdiag - jnp.diag(jnp.sum(offdiag, axis=1))


def tree_sum(values):
    for axis in ("gx", "gy"):
        peers = lax.axis_size(axis)
        low = 0
        while (1 << low) < peers:
            bits = 2 if (1 << (low + 2)) <= peers else 1
            parts = [values] + [
                lax.ppermute(values, axis, [(i, i ^ (d << low)) for i in range(peers)])
                for d in range(1, 1 << bits)
            ]
            while len(parts) > 1:
                parts = [parts[k] + parts[k + 1] for k in range(0, len(parts), 2)]
            values = parts[0]
            low += bits
    return values


def local(
    density, drift, kill, diffusion, jump_rate, kernel_vals, jump_len, rate_table, rate_index
):
    regimes, y_rows, x_cols = density.shape
    groups = lax.axis_size("gx")
    length = x_cols * groups
    per_dev = regimes * y_rows // groups
    width_a, width_b = factor_pair(length)
    tables = (
        angle_table(width_a, width_a, width_a),
        angle_table(width_b, width_b, width_b),
        angle_table(width_a, width_b, length),
    )
    support = kernel_vals.shape[1]
    inside = lax.broadcasted_iota(jnp.int32, (regimes, support), 1) < jump_len[:, None]
    weights = jnp.where(inside, kernel_vals, jnp.zeros_like(kernel_vals))
    weights = weights / jnp.sum(weights, axis=1, keepdims=True)

    def pad_lines(rows):
        return jnp.pad(rows, ((0, 0), (1, length - support - 1)))

    first_line = lax.axis_index("gx") * per_dev
    line_rates = jnp.take(jump_rate, (first_line + lax.iota(jnp.int32, per_dev)) // y_rows)
    if y_rows % per_dev == 0:
        own = pad_lines(lax.dynamic_slice_in_dim(weights, first_line // y_rows, 1, axis=0))
        own_re, own_im = forward_lines(own, tables)
        line_re = jnp.broadcast_to(own_re / length, (per_dev,) + own_re.shape[1:])
        line_im = jnp.broadcast_to(own_im / length, (per_dev,) + own_im.shape[1:])
    else:
        kern_re, kern_im = forward_lines(pad_lines(weights), tables)
        line_ids = first_line + lax.iota(jnp.int32, per_dev)
        owner_mask = (line_ids // y_rows)[:, None] == lax.iota(jnp.int32, regimes)[None, :]
        select = owner_mask.astype(jnp.float32)
        line_re = jnp.einsum("lr,rkj->lkj", select, kern_re / length, precision=HIGHEST_PRECISION)
        line_im = jnp.einsum("lr,rkj->lkj", select, kern_im / length, precision=HIGHEST_PRECISION)
    generator_matrix = generator(rate_table, rate_index)
    scale_diff = diffusion[:, None, None]
    scale_jump = jump_rate[:, None, None]
    field = density
    sums = []
    for sweep_index in range(SWEEPS):
        line_data = lax.all_to_all(
            field.reshape(regimes * y_rows, x_cols), "gx", split_axis=0, concat_axis=1, tiled=True
        )
        spec_re, spec_im = forward_lines(line_data, tables)
        prod_re = spec_re * line_re - spec_im * line_im
        prod_im = spec_re * line_im + spec_im * line_re
        jump_line = inverse_lines(prod_re, prod_im, tables)
        mixing = jnp.einsum("rs,ryx->syx", generator_matrix, field, precision=HIGHEST_PRECISION)
        jumped = lax.all_to_all(jump_line, "gx", split_axis=1, concat_axis=0, tiled=True).reshape(
            regimes, y_rows, x_cols
        )
        beside_x = with_halo(jnp.stack([field, drift[0][None] * field]), (("gx", 3),), 1)
        beside_y = with_halo(jnp.stack([field, drift[1][None] * field]), (("gy", 2),), 1)
        laplace = (
            beside_x[0][:, :, 2:]
            + beside_x[0][:, :, :-2]
            + beside_y[0][:, 2:, :]
            + beside_y[0][:, :-2, :]
            - 4.0 * field
        )
        flow_x = (beside_x[1][:, :, 2:] - beside_x[1][:, :, :-2]) * 0.5
        flow_y = (beside_y[1][:, 2:, :] - beside_y[1][:, :-2, :]) * 0.5
        updated = (
            field
            + scale_diff * laplace
            - flow_x
            - flow_y
            + scale_jump * (jumped - field)
            - kill[None] * field
            + mixing
        )
        rest = (
            field
            + scale_diff * laplace
            - flow_x
            - flow_y
            - scale_jump * field
            - kill[None] * field
            + mixing
        )
        jump_mass = length * (spec_re[:, 0, 0] * line_re[:, 0, 0] - spec_im[:, 0, 0] * line_im[:, 0, 0])
        sums.append(jnp.sum(rest) + jnp.sum(line_rates * jump_mass))
        field = updated
    cell_count = field.size * lax.axis_size("gx") * lax.axis_size("gy")
    totals = tree_sum(jnp.broadcast_to(jnp.stack(sums)[:, None], (len(sums), 128)))[:, 0]
    scale = jnp.float32(1.0)
    for sweep_index in range(SWEEPS):
        mass_mean = totals[sweep_index] / scale / cell_count
        if sweep_index == SWEEPS - 1:
            field = field / scale / mass_mean
        scale = scale * mass_mean
    return field


def solution(mesh):
    return jax.shard_map(
        local,
        mesh=mesh,
        in_specs=(
            P(None, "gy", "gx"),
            P(None, "gy", "gx"),
            P("gy", "gx"),
            P(),
            P(),
            P(),
            P(),
            P(),
            P(),
        ),
        out_specs=P(None, "gy", "gx"),
        check_vma=False,
    )
```

```python
import math

import jax
import jax.numpy as jnp
from jax import lax
from jax.sharding import PartitionSpec as P

SWEEPS = 2


HIGHEST_PRECISION = lax.Precision.HIGH


def with_halo(array, sides, width):
    for axis, dim in sides:
        peers, length = (lax.axis_size(axis), array.shape[dim])
        up = [(i, (i + 1) % peers) for i in range(peers)]
        down = [(j, i) for i, j in up]
        last = lax.slice_in_dim(array, length - width, length, axis=dim)
        leading = lax.slice_in_dim(array, 0, width, axis=dim)
        before = lax.ppermute(last, axis, up)
        after = lax.ppermute(leading, axis, down)
        array = jnp.concatenate([before, array, after], axis=dim)
    return array


def angle_table(height, breadth, period):
    product = (
        lax.broadcasted_iota(jnp.int32, (height, breadth), 0)
        * lax.broadcasted_iota(jnp.int32, (height, breadth), 1)
        % period
    )
    angles = product.astype(jnp.float32) * (2.0 * math.pi / period)
    return (jnp.cos(angles), jnp.sin(angles))


def factor_pair(length):
    low_factor = 1
    factor = 1
    while factor * factor <= length:
        if length % factor == 0:
            low_factor = factor
        factor += 1
    return (low_factor, length // low_factor)


def forward_lines(line_data, tables):
    (cos_a, sin_a), (cos_b, sin_b), (cos_t, sin_t) = tables
    width_a = cos_a.shape[0]
    width_b = cos_b.shape[0]
    line_count = line_data.shape[0]
    blocks = line_data.reshape(line_count, width_a, width_b)
    table_a = jnp.concatenate([cos_a, -sin_a], axis=1)
    first = jnp.einsum("mab,ak->mkb", blocks, table_a, precision=HIGHEST_PRECISION)
    first_re, first_im = first[:, :width_a], first[:, width_a:]
    turned_re = first_re * cos_t + first_im * sin_t
    turned_im = first_im * cos_t - first_re * sin_t
    table_b = jnp.concatenate(
        [jnp.concatenate([cos_b, -sin_b], axis=1), jnp.concatenate([sin_b, cos_b], axis=1)], axis=0
    )
    turned = jnp.concatenate([turned_re, turned_im], axis=2)
    final = jnp.einsum("mkb,bj->mkj", turned, table_b, precision=HIGHEST_PRECISION)
    return (final[:, :, :width_b], final[:, :, width_b:])


def inverse_lines(spec_re, spec_im, tables):
    (cos_a, sin_a), (cos_b, sin_b), (cos_t, sin_t) = tables
    line_count, width_a, width_b = spec_re.shape
    table_b = jnp.concatenate(
        [jnp.concatenate([cos_b, sin_b], axis=1), jnp.concatenate([-sin_b, cos_b], axis=1)], axis=0
    )
    back = jnp.einsum(
        "mkj,jb->mkb", jnp.concatenate([spec_re, spec_im], axis=2), table_b,
        precision=HIGHEST_PRECISION,
    )
    back_re, back_im = back[:, :, :width_b], back[:, :, width_b:]
    turned_re = back_re * cos_t - back_im * sin_t
    turned_im = back_re * sin_t + back_im * cos_t
    table_a = jnp.concatenate([cos_a, -sin_a], axis=0)
    result = jnp.einsum(
        "mkb,ka->mab", jnp.concatenate([turned_re, turned_im], axis=1), table_a,
        precision=HIGHEST_PRECISION,
    )
    return result.reshape(line_count, width_a * width_b)


def generator(rate_table, rate_index):
    regimes = rate_index.shape[0]
    entries = rate_table.shape[0]
    picked = (rate_index[:, :, None] == lax.iota(jnp.int32, entries)[None, None, :]).astype(
        jnp.float32
    )
    offdiag = jnp.sum(picked * rate_table[None, None, :], axis=2) * (
        1.0 - jnp.eye(regimes, dtype=jnp.float32)
    )
    return offdiag - jnp.diag(jnp.sum(offdiag, axis=1))


def tree_sum(values):
    for axis in ("gx", "gy"):
        peers = lax.axis_size(axis)
        low = 0
        while (1 << low) < peers:
            bits = 2 if (1 << (low + 2)) <= peers else 1
            parts = [values] + [
                lax.ppermute(values, axis, [(i, i ^ (d << low)) for i in range(peers)])
                for d in range(1, 1 << bits)
            ]
            while len(parts) > 1:
                parts = [parts[k] + parts[k + 1] for k in range(0, len(parts), 2)]
            values = parts[0]
            low += bits
    return values


def local(
    density, drift, kill, diffusion, jump_rate, kernel_vals, jump_len, rate_table, rate_index
):
    regimes, y_rows, x_cols = density.shape
    groups = lax.axis_size("gx")
    length = x_cols * groups
    per_dev = regimes * y_rows // groups
    width_a, width_b = factor_pair(length)
    tables = (
        angle_table(width_a, width_a, width_a),
        angle_table(width_b, width_b, width_b),
        angle_table(width_a, width_b, length),
    )
    support = kernel_vals.shape[1]
    inside = lax.broadcasted_iota(jnp.int32, (regimes, support), 1) < jump_len[:, None]
    weights = jnp.where(inside, kernel_vals, jnp.zeros_like(kernel_vals))
    weights = weights / jnp.sum(weights, axis=1, keepdims=True)

    def pad_lines(rows):
        return jnp.pad(rows, ((0, 0), (1, length - support - 1)))

    first_line = lax.axis_index("gx") * per_dev
    line_rates = jnp.take(jump_rate, (first_line + lax.iota(jnp.int32, per_dev)) // y_rows)
    if y_rows % per_dev == 0:
        own = pad_lines(lax.dynamic_slice_in_dim(weights, first_line // y_rows, 1, axis=0))
        own_re, own_im = forward_lines(own, tables)
        line_re = jnp.broadcast_to(own_re / length, (per_dev,) + own_re.shape[1:])
        line_im = jnp.broadcast_to(own_im / length, (per_dev,) + own_im.shape[1:])
    else:
        kern_re, kern_im = forward_lines(pad_lines(weights), tables)
        line_ids = first_line + lax.iota(jnp.int32, per_dev)
        owner_mask = (line_ids // y_rows)[:, None] == lax.iota(jnp.int32, regimes)[None, :]
        select = owner_mask.astype(jnp.float32)
        line_re = jnp.einsum("lr,rkj->lkj", select, kern_re / length, precision=HIGHEST_PRECISION)
        line_im = jnp.einsum("lr,rkj->lkj", select, kern_im / length, precision=HIGHEST_PRECISION)
    generator_matrix = generator(rate_table, rate_index)
    scale_diff = diffusion[:, None, None]
    scale_jump = jump_rate[:, None, None]
    field = density
    sums = []
    for sweep_index in range(SWEEPS):
        line_data = lax.all_to_all(
            field.reshape(regimes * y_rows, x_cols), "gx", split_axis=0, concat_axis=1, tiled=True
        )
        spec_re, spec_im = forward_lines(line_data, tables)
        prod_re = spec_re * line_re - spec_im * line_im
        prod_im = spec_re * line_im + spec_im * line_re
        jump_line = inverse_lines(prod_re, prod_im, tables)
        mixing = jnp.sum(generator_matrix[:, :, None, None] * field[:, None], axis=0)
        jumped = lax.all_to_all(jump_line, "gx", split_axis=1, concat_axis=0, tiled=True).reshape(
            regimes, y_rows, x_cols
        )
        beside_x = with_halo(jnp.stack([field, drift[0][None] * field]), (("gx", 3),), 1)
        beside_y = with_halo(jnp.stack([field, drift[1][None] * field]), (("gy", 2),), 1)
        laplace = (
            beside_x[0][:, :, 2:]
            + beside_x[0][:, :, :-2]
            + beside_y[0][:, 2:, :]
            + beside_y[0][:, :-2, :]
            - 4.0 * field
        )
        flow_x = (beside_x[1][:, :, 2:] - beside_x[1][:, :, :-2]) * 0.5
        flow_y = (beside_y[1][:, 2:, :] - beside_y[1][:, :-2, :]) * 0.5
        updated = (
            field
            + scale_diff * laplace
            - flow_x
            - flow_y
            + scale_jump * (jumped - field)
            - kill[None] * field
            + mixing
        )
        rest = (
            field
            + scale_diff * laplace
            - flow_x
            - flow_y
            - scale_jump * field
            - kill[None] * field
            + mixing
        )
        jump_mass = length * (spec_re[:, 0, 0] * line_re[:, 0, 0] - spec_im[:, 0, 0] * line_im[:, 0, 0])
        sums.append(jnp.sum(rest) + jnp.sum(line_rates * jump_mass))
        field = updated
    cell_count = field.size * lax.axis_size("gx") * lax.axis_size("gy")
    totals = tree_sum(jnp.broadcast_to(jnp.stack(sums)[:, None], (len(sums), 128)))[:, 0]
    scale = jnp.float32(1.0)
    for sweep_index in range(SWEEPS):
        mass_mean = totals[sweep_index] / scale / cell_count
        if sweep_index == SWEEPS - 1:
            field = field / scale / mass_mean
        scale = scale * mass_mean
    return field


def solution(mesh):
    return jax.shard_map(
        local,
        mesh=mesh,
        in_specs=(
            P(None, "gy", "gx"),
            P(None, "gy", "gx"),
            P("gy", "gx"),
            P(),
            P(),
            P(),
            P(),
            P(),
            P(),
        ),
        out_specs=P(None, "gy", "gx"),
        check_vma=False,
    )
```

```python
import math

import jax
import jax.numpy as jnp
from jax import lax
from jax.sharding import PartitionSpec as P

SWEEPS = 2


HIGHEST_PRECISION = lax.Precision.HIGH


def with_halo(array, sides, width):
    for axis, dim in sides:
        peers, length = (lax.axis_size(axis), array.shape[dim])
        up = [(i, (i + 1) % peers) for i in range(peers)]
        down = [(j, i) for i, j in up]
        last = lax.slice_in_dim(array, length - width, length, axis=dim)
        leading = lax.slice_in_dim(array, 0, width, axis=dim)
        before = lax.ppermute(last, axis, up)
        after = lax.ppermute(leading, axis, down)
        array = jnp.concatenate([before, array, after], axis=dim)
    return array


def angle_table(height, breadth, period):
    product = (
        lax.broadcasted_iota(jnp.int32, (height, breadth), 0)
        * lax.broadcasted_iota(jnp.int32, (height, breadth), 1)
        % period
    )
    angles = product.astype(jnp.float32) * (2.0 * math.pi / period)
    return (jnp.cos(angles), jnp.sin(angles))


def factor_pair(length):
    low_factor = 1
    factor = 1
    while factor * factor <= length:
        if length % factor == 0:
            low_factor = factor
        factor += 1
    return (low_factor, length // low_factor)


def forward_lines(line_data, tables):
    (cos_a, sin_a), (cos_b, sin_b), (cos_t, sin_t) = tables
    width_a = cos_a.shape[0]
    width_b = cos_b.shape[0]
    line_count = line_data.shape[0]
    blocks = line_data.reshape(line_count, width_a, width_b)
    table_a = jnp.concatenate([cos_a, -sin_a], axis=1)
    first = jnp.einsum("mab,ak->mkb", blocks, table_a, precision=HIGHEST_PRECISION)
    first_re, first_im = first[:, :width_a], first[:, width_a:]
    turned_re = first_re * cos_t + first_im * sin_t
    turned_im = first_im * cos_t - first_re * sin_t
    table_b = jnp.concatenate(
        [jnp.concatenate([cos_b, -sin_b], axis=1), jnp.concatenate([sin_b, cos_b], axis=1)], axis=0
    )
    turned = jnp.concatenate([turned_re, turned_im], axis=2)
    final = jnp.einsum("mkb,bj->mkj", turned, table_b, precision=HIGHEST_PRECISION)
    return (final[:, :, :width_b], final[:, :, width_b:])


def inverse_lines(spec_re, spec_im, tables):
    (cos_a, sin_a), (cos_b, sin_b), (cos_t, sin_t) = tables
    line_count, width_a, width_b = spec_re.shape
    table_b = jnp.concatenate(
        [jnp.concatenate([cos_b, sin_b], axis=1), jnp.concatenate([-sin_b, cos_b], axis=1)], axis=0
    )
    back = jnp.einsum(
        "mkj,jb->mkb", jnp.concatenate([spec_re, spec_im], axis=2), table_b,
        precision=HIGHEST_PRECISION,
    )
    back_re, back_im = back[:, :, :width_b], back[:, :, width_b:]
    turned_re = back_re * cos_t - back_im * sin_t
    turned_im = back_re * sin_t + back_im * cos_t
    table_a = jnp.concatenate([cos_a, -sin_a], axis=0)
    result = jnp.einsum(
        "mkb,ka->mab", jnp.concatenate([turned_re, turned_im], axis=1), table_a,
        precision=HIGHEST_PRECISION,
    )
    return result.reshape(line_count, width_a * width_b)


def generator(rate_table, rate_index):
    regimes = rate_index.shape[0]
    entries = rate_table.shape[0]
    picked = (rate_index[:, :, None] == lax.iota(jnp.int32, entries)[None, None, :]).astype(
        jnp.float32
    )
    offdiag = jnp.sum(picked * rate_table[None, None, :], axis=2) * (
        1.0 - jnp.eye(regimes, dtype=jnp.float32)
    )
    return offdiag - jnp.diag(jnp.sum(offdiag, axis=1))


def tree_sum(values):
    for axis in ("gx", "gy"):
        peers = lax.axis_size(axis)
        low = 0
        while (1 << low) < peers:
            bits = 2 if (1 << (low + 2)) <= peers else 1
            parts = [values] + [
                lax.ppermute(values, axis, [(i, i ^ (d << low)) for i in range(peers)])
                for d in range(1, 1 << bits)
            ]
            while len(parts) > 1:
                parts = [parts[k] + parts[k + 1] for k in range(0, len(parts), 2)]
            values = parts[0]
            low += bits
    return values


def local(
    density, drift, kill, diffusion, jump_rate, kernel_vals, jump_len, rate_table, rate_index
):
    regimes, y_rows, x_cols = density.shape
    groups = lax.axis_size("gx")
    length = x_cols * groups
    per_dev = regimes * y_rows // groups
    width_a, width_b = factor_pair(length)
    tables = (
        angle_table(width_a, width_a, width_a),
        angle_table(width_b, width_b, width_b),
        angle_table(width_a, width_b, length),
    )
    support = kernel_vals.shape[1]
    inside = lax.broadcasted_iota(jnp.int32, (regimes, support), 1) < jump_len[:, None]
    weights = jnp.where(inside, kernel_vals, jnp.zeros_like(kernel_vals))
    weights = weights / jnp.sum(weights, axis=1, keepdims=True)

    def pad_lines(rows):
        return jnp.pad(rows, ((0, 0), (1, length - support - 1)))

    first_line = lax.axis_index("gx") * per_dev
    kernel_mass = jnp.sum(weights, axis=1)
    if y_rows % per_dev == 0:
        own = pad_lines(lax.dynamic_slice_in_dim(weights, first_line // y_rows, 1, axis=0))
        own_re, own_im = forward_lines(own, tables)
        line_re = jnp.broadcast_to(own_re / length, (per_dev,) + own_re.shape[1:])
        line_im = jnp.broadcast_to(own_im / length, (per_dev,) + own_im.shape[1:])
    else:
        kern_re, kern_im = forward_lines(pad_lines(weights), tables)
        line_ids = first_line + lax.iota(jnp.int32, per_dev)
        owner_mask = (line_ids // y_rows)[:, None] == lax.iota(jnp.int32, regimes)[None, :]
        select = owner_mask.astype(jnp.float32)
        line_re = jnp.einsum("lr,rkj->lkj", select, kern_re / length, precision=HIGHEST_PRECISION)
        line_im = jnp.einsum("lr,rkj->lkj", select, kern_im / length, precision=HIGHEST_PRECISION)
    generator_matrix = generator(rate_table, rate_index)
    scale_diff = diffusion[:, None, None]
    scale_jump = jump_rate[:, None, None]
    field = density
    sums = []
    for sweep_index in range(SWEEPS):
        line_data = lax.all_to_all(
            field.reshape(regimes * y_rows, x_cols), "gx", split_axis=0, concat_axis=1, tiled=True
        )
        spec_re, spec_im = forward_lines(line_data, tables)
        prod_re = spec_re * line_re - spec_im * line_im
        prod_im = spec_re * line_im + spec_im * line_re
        jump_line = inverse_lines(prod_re, prod_im, tables)
        mixing = jnp.einsum("rs,ryx->syx", generator_matrix, field, precision=HIGHEST_PRECISION)
        jumped = lax.all_to_all(jump_line, "gx", split_axis=1, concat_axis=0, tiled=True).reshape(
            regimes, y_rows, x_cols
        )
        beside_x = with_halo(jnp.stack([field, drift[0][None] * field]), (("gx", 3),), 1)
        beside_y = with_halo(jnp.stack([field, drift[1][None] * field]), (("gy", 2),), 1)
        laplace = (
            beside_x[0][:, :, 2:]
            + beside_x[0][:, :, :-2]
            + beside_y[0][:, 2:, :]
            + beside_y[0][:, :-2, :]
            - 4.0 * field
        )
        flow_x = (beside_x[1][:, :, 2:] - beside_x[1][:, :, :-2]) * 0.5
        flow_y = (beside_y[1][:, 2:, :] - beside_y[1][:, :-2, :]) * 0.5
        updated = (
            field
            + scale_diff * laplace
            - flow_x
            - flow_y
            + scale_jump * (jumped - field)
            - kill[None] * field
            + mixing
        )
        rest = (
            field
            + scale_diff * laplace
            - flow_x
            - flow_y
            - scale_jump * field
            - kill[None] * field
            + mixing
        )
        jump_mass = kernel_mass * jnp.sum(field, axis=(1, 2))
        sums.append(jnp.sum(rest) + jnp.sum(jump_rate * jump_mass))
        field = updated
    cell_count = field.size * lax.axis_size("gx") * lax.axis_size("gy")
    totals = tree_sum(jnp.broadcast_to(jnp.stack(sums)[:, None], (len(sums), 128)))[:, 0]
    scale = jnp.float32(1.0)
    for sweep_index in range(SWEEPS):
        mass_mean = totals[sweep_index] / scale / cell_count
        if sweep_index == SWEEPS - 1:
            field = field / scale / mass_mean
        scale = scale * mass_mean
    return field


def solution(mesh):
    return jax.shard_map(
        local,
        mesh=mesh,
        in_specs=(
            P(None, "gy", "gx"),
            P(None, "gy", "gx"),
            P("gy", "gx"),
            P(),
            P(),
            P(),
            P(),
            P(),
            P(),
        ),
        out_specs=P(None, "gy", "gx"),
        check_vma=False,
    )
```

```python
import math

import jax
import jax.numpy as jnp
from jax import lax
from jax.sharding import PartitionSpec as P


SWEEPS = 2


HIGHEST_PRECISION = lax.Precision.HIGH


def with_halo(array, sides, width):
    for axis, dim in sides:
        peers, length = (lax.axis_size(axis), array.shape[dim])
        up = [(i, (i + 1) % peers) for i in range(peers)]
        down = [(j, i) for i, j in up]
        last = lax.slice_in_dim(array, length - width, length, axis=dim)
        leading = lax.slice_in_dim(array, 0, width, axis=dim)
        before = lax.ppermute(last, axis, up)
        after = lax.ppermute(leading, axis, down)
        array = jnp.concatenate([before, array, after], axis=dim)
    return array


def angle_table(height, breadth, period):
    product = (
        lax.broadcasted_iota(jnp.int32, (height, breadth), 0)
        * lax.broadcasted_iota(jnp.int32, (height, breadth), 1)
        % period
    )
    angles = product.astype(jnp.float32) * (2.0 * math.pi / period)
    return (jnp.cos(angles), jnp.sin(angles))


def factor_pair(length):
    low_factor = 1
    factor = 1
    while factor * factor <= length:
        if length % factor == 0:
            low_factor = factor
        factor += 1
    return (low_factor, length // low_factor)


def forward_lines(line_data, tables):
    (cos_a, sin_a), (cos_b, sin_b), (cos_t, sin_t) = tables
    width_a = cos_a.shape[0]
    width_b = cos_b.shape[0]
    line_count = line_data.shape[0]
    rows = line_data.shape[1] // width_b
    blocks = line_data.reshape(line_count, rows, width_b)
    table_a = jnp.concatenate([cos_a, -sin_a], axis=1)[:rows]
    first = jnp.einsum("mab,ak->mkb", blocks, table_a, precision=HIGHEST_PRECISION)
    first_re, first_im = first[:, :width_a], first[:, width_a:]
    turned_re = first_re * cos_t + first_im * sin_t
    turned_im = first_im * cos_t - first_re * sin_t
    table_b = jnp.concatenate(
        [jnp.concatenate([cos_b, -sin_b], axis=1), jnp.concatenate([sin_b, cos_b], axis=1)], axis=0
    )
    turned = jnp.concatenate([turned_re, turned_im], axis=2)
    final = jnp.einsum("mkb,bj->mkj", turned, table_b, precision=HIGHEST_PRECISION)
    return (final[:, :, :width_b], final[:, :, width_b:])


def inverse_lines(spec_re, spec_im, tables):
    (cos_a, sin_a), (cos_b, sin_b), (cos_t, sin_t) = tables
    line_count, width_a, width_b = spec_re.shape
    table_b = jnp.concatenate(
        [jnp.concatenate([cos_b, sin_b], axis=1), jnp.concatenate([-sin_b, cos_b], axis=1)], axis=0
    )
    back = jnp.einsum(
        "mkj,jb->mkb", jnp.concatenate([spec_re, spec_im], axis=2), table_b,
        precision=HIGHEST_PRECISION,
    )
    back_re, back_im = back[:, :, :width_b], back[:, :, width_b:]
    turned_re = back_re * cos_t - back_im * sin_t
    turned_im = back_re * sin_t + back_im * cos_t
    table_a = jnp.concatenate([cos_a, -sin_a], axis=0)
    result = jnp.einsum(
        "mkb,ka->mab", jnp.concatenate([turned_re, turned_im], axis=1), table_a,
        precision=HIGHEST_PRECISION,
    )
    return result.reshape(line_count, width_a * width_b)


def generator(rate_table, rate_index):
    regimes = rate_index.shape[0]
    entries = rate_table.shape[0]
    picked = (rate_index[:, :, None] == lax.iota(jnp.int32, entries)[None, None, :]).astype(
        jnp.float32
    )
    offdiag = jnp.sum(picked * rate_table[None, None, :], axis=2) * (
        1.0 - jnp.eye(regimes, dtype=jnp.float32)
    )
    return offdiag - jnp.diag(jnp.sum(offdiag, axis=1))


def tree_sum(values):
    for axis in ("gx", "gy"):
        peers = lax.axis_size(axis)
        low = 0
        while (1 << low) < peers:
            bits = 2 if (1 << (low + 2)) <= peers else 1
            parts = [values] + [
                lax.ppermute(values, axis, [(i, i ^ (d << low)) for i in range(peers)])
                for d in range(1, 1 << bits)
            ]
            while len(parts) > 1:
                parts = [parts[k] + parts[k + 1] for k in range(0, len(parts), 2)]
            values = parts[0]
            low += bits
    return values


def local(
    density, drift, kill, diffusion, jump_rate, kernel_vals, jump_len, rate_table, rate_index
):
    regimes, y_rows, x_cols = density.shape
    groups = lax.axis_size("gx")
    length = x_cols * groups
    per_dev = regimes * y_rows // groups
    width_a, width_b = factor_pair(length)
    tables = (
        angle_table(width_a, width_a, width_a),
        angle_table(width_b, width_b, width_b),
        angle_table(width_a, width_b, length),
    )
    support = kernel_vals.shape[1]
    inside = lax.broadcasted_iota(jnp.int32, (regimes, support), 1) < jump_len[:, None]
    weights = jnp.where(inside, kernel_vals, jnp.zeros_like(kernel_vals))
    weights = weights / jnp.sum(weights, axis=1, keepdims=True)

    def pad_lines(rows):
        return jnp.pad(rows, ((0, 0), (1, length - support - 1)))

    first_line = lax.axis_index("gx") * per_dev
    kernel_mass = jnp.sum(weights, axis=1)
    if y_rows % per_dev == 0:
        rows = min(-(-(support + 1) // width_b), width_a)
        own = jnp.pad(
            lax.dynamic_slice_in_dim(weights, first_line // y_rows, 1, axis=0),
            ((0, 0), (1, rows * width_b - support - 1)),
        )
        own_re, own_im = forward_lines(own, tables)
        line_re = jnp.broadcast_to(own_re / length, (per_dev,) + own_re.shape[1:])
        line_im = jnp.broadcast_to(own_im / length, (per_dev,) + own_im.shape[1:])
    else:
        kern_re, kern_im = forward_lines(pad_lines(weights), tables)
        line_ids = first_line + lax.iota(jnp.int32, per_dev)
        owner_mask = (line_ids // y_rows)[:, None] == lax.iota(jnp.int32, regimes)[None, :]
        select = owner_mask.astype(jnp.float32)
        line_re = jnp.einsum("lr,rkj->lkj", select, kern_re / length, precision=HIGHEST_PRECISION)
        line_im = jnp.einsum("lr,rkj->lkj", select, kern_im / length, precision=HIGHEST_PRECISION)
    generator_matrix = generator(rate_table, rate_index)
    scale_diff = diffusion[:, None, None]
    scale_jump = jump_rate[:, None, None]
    field = density
    sums = []
    for _ in range(SWEEPS):
        line_data = lax.all_to_all(
            field.reshape(regimes * y_rows, x_cols), "gx", split_axis=0, concat_axis=1, tiled=True
        )
        spec_re, spec_im = forward_lines(line_data, tables)
        prod_re = spec_re * line_re - spec_im * line_im
        prod_im = spec_re * line_im + spec_im * line_re
        jump_line = inverse_lines(prod_re, prod_im, tables)
        mixing = jnp.einsum("rs,ryx->syx", generator_matrix, field, precision=HIGHEST_PRECISION)
        jumped = lax.all_to_all(jump_line, "gx", split_axis=1, concat_axis=0, tiled=True).reshape(
            regimes, y_rows, x_cols
        )
        beside_x = with_halo(jnp.stack([field, drift[0][None] * field]), (("gx", 3),), 1)
        beside_y = with_halo(jnp.stack([field, drift[1][None] * field]), (("gy", 2),), 1)
        laplace = (
            beside_x[0][:, :, 2:]
            + beside_x[0][:, :, :-2]
            + beside_y[0][:, 2:, :]
            + beside_y[0][:, :-2, :]
            - 4.0 * field
        )
        flow_x = (beside_x[1][:, :, 2:] - beside_x[1][:, :, :-2]) * 0.5
        flow_y = (beside_y[1][:, 2:, :] - beside_y[1][:, :-2, :]) * 0.5
        updated = (
            field
            + scale_diff * laplace
            - flow_x
            - flow_y
            + scale_jump * (jumped - field)
            - kill[None] * field
            + mixing
        )
        rest = (
            field
            + scale_diff * laplace
            - flow_x
            - flow_y
            - scale_jump * field
            - kill[None] * field
            + mixing
        )
        jump_mass = kernel_mass * jnp.sum(field, axis=(1, 2))
        sums.append(jnp.sum(rest) + jnp.sum(jump_rate * jump_mass))
        field = updated
    cell_count = field.size * lax.axis_size("gx") * lax.axis_size("gy")
    totals = tree_sum(jnp.broadcast_to(jnp.stack(sums)[:, None], (len(sums), 128)))[:, 0]
    scale = jnp.float32(1.0)
    for sweep_index in range(SWEEPS):
        mass_mean = totals[sweep_index] / scale / cell_count
        if sweep_index == SWEEPS - 1:
            field = field / scale / mass_mean
        scale = scale * mass_mean
    return field


def solution(mesh):
    return jax.shard_map(
        local,
        mesh=mesh,
        in_specs=(
            P(None, "gy", "gx"),
            P(None, "gy", "gx"),
            P("gy", "gx"),
            P(),
            P(),
            P(),
            P(),
            P(),
            P(),
        ),
        out_specs=P(None, "gy", "gx"),
        check_vma=False,
    )
```
